32 devices in a mesh: inner: 8 (over y, x, core), outer: 4 (over z).
Axes of the slice: x: 2, y: 2, z: 4, core: 2. Of those that a mesh axis runs over, the one named last changes fastest.
Arguments:
- query_rows: bfloat16 [8, 1024, 1024], P('inner', 'outer'), may hold values from -120 to 120
- key_rows: bfloat16 [8, 1024, 128], P('inner', 'outer'), may hold values from -6 to 6
- value_rows: bfloat16 [8, 1024, 128], P('inner', 'outer'), may hold values from -6 to 6
- out_grad: bfloat16 [8, 1024, 1024], P('inner', 'outer'), may hold values from -6 to 6
- doc_start: int32 [8, 1024], P('inner', 'outer'), may hold values from 0 to 8191, as said below
Outputs:
- query_grad: bfloat16 [8, 1024, 1024], P('inner', 'outer')
- key_grad: bfloat16 [8, 1024, 128], P('inner', 'outer')
- value_grad: bfloat16 [8, 1024, 128], P('inner', 'outer')
The draws below stay inside these ranges and needn't reach their ends.
Inputs may be any that keep to these rules, and one draw needn't show every extreme that they name: doc_start[p] <= p, doc_start never falls along the sequence, and doc_start[doc_start[p]] = doc_start[p]; the tokens at position 0 and at the last position each start a document.
All inputs are finite; a program needn't handle non-finite values.
Results may differ from the reference program's by a relative error of at most 0.0075.
Values may be sent and summed in bfloat16 or wider, within the bound.
A program may use at most 64 MiB of HBM per device.

```python
import jax
import jax.numpy as jnp
from jax import lax

HQ = 8
HD = 128
TOK_DEV = 256
GROUPS = 8
GROUP = 1024
SEQ = 8192
WIN = 512
DOC_MEAN = 512


def query_key_pair(key):
    keys = jnp.clip(jax.random.normal(jax.random.fold_in(key, 101), (SEQ, HD), jnp.float32), -6.0, 6.0)
    queries = jnp.clip(jax.random.normal(jax.random.fold_in(key, 102), (SEQ, HQ, HD), jnp.float32), -6.0, 6.0)
    return (queries.reshape(GROUPS, GROUP, HQ * HD), keys.reshape(GROUPS, GROUP, HD))


def draw_query_rows(key, part):
    return query_key_pair(key)[0].astype(jnp.bfloat16)


def draw_key_rows(key, part):
    return query_key_pair(key)[1].astype(jnp.bfloat16)


def draw_doc_start(key, part):
    position = jnp.arange(SEQ, dtype=jnp.int32)
    opening = jax.random.randint(key, (SEQ,), 0, DOC_MEAN) == 0
    opening = opening | (position == 0) | (position == SEQ - 1)
    starts = lax.cummax(jnp.where(opening, position, 0), axis=0)
    return starts.reshape(GROUPS, GROUP)


def level_of(own_key, dims, shards, least, top_value):
    def one(axis_at, shards_of):
        draws = jax.random.uniform(jax.random.fold_in(jax.random.fold_in(own_key, 6), axis_at), (shards_of,), jnp.float32, least / len(shards), top_value / len(shards))
        return jnp.repeat(jnp.exp(draws), dims[axis_at] // shards_of).reshape((-1,) + (1,) * (len(dims) - axis_at - 1))

    loudness = one(*shards[0])
    for cut in shards[1:]:
        loudness = loudness * one(*cut)
    return loudness


def scatter_about(rng, extent, width, bound, pieces=(), kind=jnp.bfloat16):
    result = jax.random.normal(rng, extent, jnp.float32) * width
    if len(pieces) > 0:
        result = level_of(rng, extent, pieces, -0.22, 0.18) * result
    return jnp.clip(result, min=-bound, max=bound).astype(kind)


def setup_inputs(seed: int = 0) -> dict:
    key_of = jax.random.split(jax.random.key(seed), 6)
    query_rows = draw_query_rows(jax.random.fold_in(key_of[5], 71), 0)
    key_rows = draw_key_rows(jax.random.fold_in(key_of[5], 71), 0)
    value_rows = scatter_about(key_of[2], (GROUPS, GROUP, HD), 1.0, 6.0, ((0, 8), (1, 4)))
    out_grad = scatter_about(key_of[3], (GROUPS, GROUP, HQ * HD), 1.0, 6.0, ((0, 8), (1, 4)))
    doc_start = draw_doc_start(jax.random.fold_in(key_of[5], 71), 0)
    return dict(query_rows=query_rows, key_rows=key_rows, value_rows=value_rows, out_grad=out_grad, doc_start=doc_start)


NEG_FILL = -1.0e30


def block_terms(block, query_flat, key_padded, value_padded, grad_flat, start_flat):
    length = TOK_DEV
    first_pos = block * length
    query_block = lax.dynamic_slice_in_dim(query_flat, first_pos, length, 0).reshape(length, HQ, HD).astype(jnp.float32)
    grad_block = lax.dynamic_slice_in_dim(grad_flat, first_pos, length, 0).reshape(length, HQ, HD).astype(jnp.float32)
    key_window = lax.dynamic_slice_in_dim(key_padded, first_pos, 3 * length, 0).astype(jnp.float32)
    value_window = lax.dynamic_slice_in_dim(value_padded, first_pos, 3 * length, 0).astype(jnp.float32)
    starts = lax.dynamic_slice_in_dim(start_flat, first_pos, length, 0)
    query_pos = first_pos + jnp.arange(length, dtype=jnp.int32)
    key_pos = first_pos - 2 * length + jnp.arange(3 * length, dtype=jnp.int32)
    keep_mask = (key_pos[None, :] <= query_pos[:, None]) & (key_pos[None, :] > query_pos[:, None] - WIN) & (key_pos[None, :] >= starts[:, None])
    score_scale = HD ** -0.5
    scores = jnp.einsum("thd,kd->htk", query_block, key_window) * score_scale
    scores = jnp.where(keep_mask[None], scores, NEG_FILL)
    row_top = jnp.max(scores, axis=-1, keepdims=True)
    weights = jnp.exp(scores - row_top)
    row_total = jnp.sum(weights, axis=-1, keepdims=True)
    probability = weights / row_total
    prob_low = lax.optimization_barrier(probability.astype(jnp.bfloat16)).astype(jnp.float32)
    output = jnp.einsum("htk,kd->thd", prob_low, value_window)
    row_delta = jnp.sum(grad_block * output, axis=-1)
    prob_grad = jnp.einsum("thd,kd->htk", grad_block, value_window)
    score_grad = probability * (prob_grad - row_delta.T[:, :, None]) * score_scale
    score_low = lax.optimization_barrier(score_grad.astype(jnp.bfloat16)).astype(jnp.float32)
    query_part = jnp.einsum("htk,kd->thd", score_low, key_window).reshape(length, HQ * HD).astype(jnp.bfloat16)
    key_part = jnp.einsum("htk,thd->kd", score_low, query_block)
    value_part = jnp.einsum("htk,thd->kd", prob_low, grad_block)
    return query_part, key_part, value_part


def assemble(parts):
    blocks = parts.shape[0]
    length = TOK_DEV
    tiles = parts.reshape(blocks, 3, length, HD)
    own_part = tiles[:, 2]
    next_part = jnp.concatenate([tiles[1:, 1], jnp.zeros((1, length, HD), jnp.float32)], axis=0)
    after_part = jnp.concatenate([tiles[2:, 0], jnp.zeros((2, length, HD), jnp.float32)], axis=0)
    summed = own_part + next_part + after_part
    return summed.reshape(GROUPS, GROUP, HD).astype(jnp.bfloat16)


def reference(query_rows, key_rows, value_rows, out_grad, doc_start):
    length = TOK_DEV
    query_flat = query_rows.reshape(SEQ, HQ * HD)
    grad_flat = out_grad.reshape(SEQ, HQ * HD)
    padding = jnp.zeros((2 * length, HD), key_rows.dtype)
    key_padded = jnp.concatenate([padding, key_rows.reshape(SEQ, HD)], axis=0)
    value_padded = jnp.concatenate([padding, value_rows.reshape(SEQ, HD)], axis=0)
    start_flat = doc_start.reshape(SEQ).astype(jnp.int32)
    blocks = jnp.arange(SEQ // length, dtype=jnp.int32)

    def one_block(block):
        return block_terms(block, query_flat, key_padded, value_padded, grad_flat, start_flat)

    query_parts, key_parts, value_parts = lax.map(one_block, blocks)
    query_grad = query_parts.reshape(GROUPS, GROUP, HQ * HD)
    return query_grad, assemble(key_parts), assemble(value_parts)
```

```python
import functools

import jax
import jax.numpy as jnp
from jax import lax
from jax.experimental import pallas as pl
from jax.experimental.pallas import tpu as pltpu
from jax.sharding import PartitionSpec as P

NEG_FILL = -1e30
LOG2E = 1.4426950408889634
VMEM_BYTES = 48 * 1024 * 1024
MESH = pl.DeviceIdType.MESH
HEADS_PER_STEP = 8
CONTRACT_LAST = (((1,), (1,)), ((), ()))


def dot_last(left, right):
    return lax.dot_general(left, right, CONTRACT_LAST, preferred_element_type=jnp.float32)


def dot(left, right):
    return jnp.dot(left, right, preferred_element_type=jnp.float32)


def kernel(
    inner_size, outer_size,
    q_ref, k_ref, v_ref, g_ref, start_ref,
    dq_ref, dk_ref, dv_ref,
    qs, gs, ks, vs, kt, bias, early, stat, prob, plow, ds, start_rows, own_sum, part, came,
    local_sem, send_sem, recv_sem,
):
    length = k_ref.shape[1]
    size = k_ref.shape[2]
    heads = q_ref.shape[2] // size
    scale = size ** (-0.5)
    blocks = inner_size * outer_size
    outer = lax.axis_index("outer")
    block = lax.axis_index("inner") * outer_size + outer

    def at(step):
        other = lax.rem(block + step + blocks, blocks)
        return (other // outer_size, lax.rem(other, outer_size))

    opens = outer == 0
    skips = jnp.logical_and(outer == outer_size - 2, block + 2 < blocks)
    passes = jnp.logical_and(outer < outer_size - 1, block >= 1)
    has_next = block + 1 < blocks

    barrier = pltpu.get_barrier_semaphore()

    def greet(step):
        pl.semaphore_signal(barrier, inc=1, device_id=at(step), device_id_type=MESH)

    pl.when(block >= 1)(lambda: greet(-1))
    pl.when(jnp.logical_and(opens, block >= 2))(lambda: greet(-2))

    loads = []

    def load(source, target):
        copy = pltpu.make_async_copy(source, target, local_sem.at[len(loads)])
        copy.start()
        loads.append(copy)

    load(start_ref, start_rows)
    load(k_ref.at[0], ks.at[pl.ds(0, length)])
    load(v_ref.at[0], vs.at[pl.ds(0, length)])
    for head in range(heads):
        load(q_ref.at[0, :, pl.ds(head * size, size)], qs.at[pl.ds(head * length, length)])
        load(g_ref.at[0, :, pl.ds(head * size, size)], gs.at[pl.ds(head * length, length)])

    own_rows, near_rows, far_rows = (pl.ds(tile * length, length) for tile in range(3))

    greeters = has_next.astype(jnp.int32) + skips.astype(jnp.int32)
    pl.when(has_next)(lambda: pl.semaphore_wait(barrier, greeters))
    sends = []

    def remote(source, target, step, give, take):
        return pltpu.make_async_remote_copy(
            src_ref=source, dst_ref=target,
            send_sem=send_sem.at[give], recv_sem=recv_sem.at[take],
            device_id=at(step), device_id_type=MESH,
        )

    def send(cond, *args):
        copy = remote(*args)
        pl.when(cond)(copy.start)
        sends.append((cond, copy))
        return copy

    key_near = send(has_next, k_ref.at[0], ks.at[near_rows], 1, 0, 0)
    key_far = send(skips, k_ref.at[0], ks.at[far_rows], 2, 2, 2)
    value_near = send(has_next, v_ref.at[0], vs.at[near_rows], 1, 1, 1)
    value_far = send(skips, v_ref.at[0], vs.at[far_rows], 2, 3, 3)

    def blank(rows):
        ks[rows] = jnp.zeros((length, size), jnp.bfloat16)
        vs[rows] = jnp.zeros((length, size), jnp.bfloat16)

    pl.when(block < 1)(lambda: blank(near_rows))
    pl.when(block < 2)(lambda: blank(far_rows))

    def no_part(slot):
        came[slot] = jnp.zeros((length, size), jnp.bfloat16)

    for tile in (1, 2):
        for kind in range(2):
            pl.when(block + tile >= blocks)(functools.partial(no_part, 2 * kind + tile - 1))

    first = block * length
    key_at = lax.broadcasted_iota(jnp.int32, (length, length), 0)
    query_at = lax.broadcasted_iota(jnp.int32, (length, length), 1)
    causal = key_at <= query_at
    loads[0].wait()
    starts = start_rows[...]
    mixed_pos = first + key_at - jnp.where(causal, 0, 2 * length)
    bias[pl.ds(0, length)] = jnp.where(mixed_pos >= starts, 0.0, NEG_FILL)
    bias[pl.ds(length, length)] = jnp.where(first - length + key_at >= starts, 0.0, NEG_FILL)

    for copy in loads[1:]:
        copy.wait()

    def split(mixed):
        is_own = lax.broadcasted_iota(jnp.int32, (length, length), 0) <= lax.broadcasted_iota(
            jnp.int32, (length, length), 1
        )
        zero = jnp.zeros_like(mixed)
        return (
            jnp.where(is_own, mixed, zero).astype(jnp.bfloat16),
            jnp.where(is_own, zero, mixed).astype(jnp.bfloat16),
        )

    def merge(own, far):
        is_own = lax.broadcasted_iota(jnp.int32, (length, length), 0) <= lax.broadcasted_iota(
            jnp.int32, (length, length), 1
        )
        return jnp.where(is_own, own, far)

    def put(target, head, mixed, near):
        columns = pl.ds(pl.multiple_of(head * length, length), length)
        own, far = split(mixed)
        target[pl.ds(0, length), columns] = own
        target[pl.ds(length, length), columns] = near.astype(jnp.bfloat16)
        target[pl.ds(2 * length, length), columns] = far

    def over_heads(body):
        def step(index, carry):
            for inside in range(HEADS_PER_STEP):
                body(index * HEADS_PER_STEP + inside)
            return carry

        lax.fori_loop(0, heads // HEADS_PER_STEP, step, 0)

    def rows_of(head):
        return pl.ds(pl.multiple_of(head * length, length), length)

    def own_tile(head):
        early[0, head] = dot_last(ks[own_rows], qs[rows_of(head)]) + bias[own_rows]
        early[2, head] = dot_last(vs[own_rows], gs[rows_of(head)])

    def near_scores(head):
        scores = dot_last(ks[near_rows], qs[rows_of(head)]) + bias[near_rows]
        top = jnp.max(scores, axis=0, keepdims=True)
        weights = jnp.exp2((scores - top) * (scale * LOG2E))
        early[1, head] = weights
        stat[head, 0:1] = top
        stat[head, 1:2] = jnp.sum(weights, axis=0, keepdims=True)

    def near_grads(head):
        early[3, head] = dot_last(vs[near_rows], gs[rows_of(head)])

    over_heads(own_tile)
    pl.when(block >= 1)(key_near.wait_recv)
    send(passes, ks.at[near_rows], ks.at[far_rows], 1, 4, 2)
    over_heads(near_scores)
    pl.when(block >= 1)(value_near.wait_recv)
    send(passes, vs.at[near_rows], vs.at[far_rows], 1, 5, 3)
    over_heads(near_grads)
    pl.when(block >= 2)(key_far.wait_recv)

    def forward(head):
        far = dot_last(ks[far_rows], qs[rows_of(head)]) + bias[own_rows]
        mixed = merge(early[0, head], far)
        near_top = stat[head, 0:1]
        top = jnp.maximum(jnp.max(mixed, axis=0, keepdims=True), near_top)
        mixed = jnp.exp2((mixed - top) * (scale * LOG2E))
        shrink = jnp.exp2((near_top - top) * (scale * LOG2E))
        total = jnp.sum(mixed, axis=0, keepdims=True) + shrink * stat[head, 1:2]
        inverse = 1.0 / total
        mixed = mixed * inverse
        near = early[1, head] * (shrink * inverse)
        prob[head, pl.ds(0, length)] = mixed
        prob[head, pl.ds(length, length)] = near
        put(plow, head, mixed, near)

    over_heads(forward)

    lead = jnp.where(opens, 1, 2)

    def back(kind, tile):
        slot = 2 * kind + tile - 1
        return remote(part.at[slot], came.at[slot], -tile, 6 + slot, 4 + slot)

    def give_back(weights, rows, kind):
        for tile in (lead, 3 - lead):
            from_rows = pl.ds(pl.multiple_of(tile * length, length), length)
            part[2 * kind + tile - 1] = dot(weights[from_rows], rows[...]).astype(jnp.bfloat16)
            pl.when(block >= tile)(back(kind, tile).start)

    def take_back(kind):
        for tile in (1, 2):
            pl.when(block + tile < blocks)(back(kind, tile).wait_recv)

    give_back(plow, gs, 0)
    pl.when(block >= 2)(value_far.wait_recv)

    def backward(head):
        mixed = merge(early[2, head], dot_last(vs[far_rows], gs[rows_of(head)]))
        near = early[3, head]
        mixed_prob = prob[head, pl.ds(0, length)]
        near_prob = prob[head, pl.ds(length, length)]
        delta = jnp.sum(mixed_prob * mixed, axis=0, keepdims=True) + jnp.sum(
            near_prob * near, axis=0, keepdims=True
        )
        put(ds, head, mixed_prob * (mixed - delta), near_prob * (near - delta))

    over_heads(backward)
    give_back(ds, qs, 1)

    own_sum[0] = dot(plow[own_rows], gs[...])
    own_sum[1] = dot(ds[own_rows], qs[...])
    kt[...] = ks[...].astype(jnp.float32).T.astype(jnp.bfloat16)

    for head in range(heads):
        turned = dot(kt[...], ds[:, pl.ds(head * length, length)]) * scale
        dq_ref[:, pl.ds(head * size, size)] = turned.T.astype(jnp.bfloat16)

    take_back(0)
    dv_ref[...] = (
        own_sum[0] + came[0].astype(jnp.float32) + came[1].astype(jnp.float32)
    ).astype(jnp.bfloat16)
    take_back(1)
    dk_ref[...] = (
        (own_sum[1] + came[2].astype(jnp.float32) + came[3].astype(jnp.float32)) * scale
    ).astype(jnp.bfloat16)
    for cond, copy in sends:
        pl.when(cond)(copy.wait_send)
    for kind in range(2):
        for tile in (1, 2):
            pl.when(block >= tile)(back(kind, tile).wait_send)


def write_out(dq_from, dk_from, dv_from, dq_ref, dk_ref, dv_ref, sem):
    pairs = ((dq_from, dq_ref), (dk_from, dk_ref), (dv_from, dv_ref))
    copies = [
        pltpu.make_async_copy(source, target.at[0], sem.at[which])
        for which, (source, target) in enumerate(pairs)
    ]
    for copy in copies:
        copy.start()
    for copy in copies:
        copy.wait()


def on_device(inner_size, outer_size, query_rows, key_rows, value_rows, out_grad, doc_start):
    length, size = key_rows.shape[1:]
    heads = query_rows.shape[2] // size
    low, wide = jnp.bfloat16, jnp.float32
    far = pl.BlockSpec(memory_space=pltpu.HBM)
    near = pl.BlockSpec(memory_space=pltpu.VMEM)
    given = (query_rows, key_rows, value_rows, out_grad, doc_start)
    results = pl.pallas_call(
        functools.partial(kernel, inner_size, outer_size),
        out_shape=(
            jax.ShapeDtypeStruct(query_rows.shape[1:], low),
            jax.ShapeDtypeStruct(key_rows.shape[1:], low),
            jax.ShapeDtypeStruct(value_rows.shape[1:], low),
        ),
        in_specs=[far] * 5,
        out_specs=(near, near, near),
        scratch_shapes=[
            pltpu.VMEM((heads * length, size), low),
            pltpu.VMEM((heads * length, size), low),
            pltpu.VMEM((3 * length, size), low),
            pltpu.VMEM((3 * length, size), low),
            pltpu.VMEM((size, 3 * length), low),
            pltpu.VMEM((2 * length, length), wide),
            pltpu.VMEM((4, heads, length, length), wide),
            pltpu.VMEM((heads, 8, length), wide),
            pltpu.VMEM((heads, 2 * length, length), wide),
            pltpu.VMEM((3 * length, heads * length), low),
            pltpu.VMEM((3 * length, heads * length), low),
            pltpu.VMEM((1, length), jnp.int32),
            pltpu.VMEM((2, length, size), wide),
            pltpu.VMEM((4, length, size), low),
            pltpu.VMEM((4, length, size), low),
            pltpu.SemaphoreType.DMA((3 + 2 * heads,)),
            pltpu.SemaphoreType.DMA((10,)),
            pltpu.SemaphoreType.DMA((8,)),
        ],
        compiler_params=pltpu.CompilerParams(
            collective_id=0, has_side_effects=True, vmem_limit_bytes=VMEM_BYTES
        ),
        name="window_attention_grad",
    )(*(pltpu.with_memory_space_constraint(rows, pltpu.HBM) for rows in given))
    return pl.pallas_call(
        write_out,
        out_shape=tuple(jax.ShapeDtypeStruct((1,) + result.shape, low) for result in results),
        in_specs=[near] * 3,
        out_specs=(far,) * 3,
        scratch_shapes=[pltpu.SemaphoreType.DMA((3,))],
        compiler_params=pltpu.CompilerParams(vmem_limit_bytes=1024 * 1024),
        name="write_out",
    )(*results)


def solution(mesh):
    rows = P("inner", "outer", None)
    return jax.shard_map(
        functools.partial(on_device, mesh.shape["inner"], mesh.shape["outer"]),
        mesh=mesh,
        in_specs=(rows, rows, rows, rows, P("inner", "outer")),
        out_specs=(rows, rows, rows),
        check_vma=False,
    )
```

```python
import functools

import jax
import jax.numpy as jnp
from jax import lax
from jax.experimental import pallas as pl
from jax.experimental.pallas import tpu as pltpu
from jax.sharding import PartitionSpec as P

NEG_FILL = -1e30
LOG2E = 1.4426950408889634
VMEM_BYTES = 48 * 1024 * 1024
MESH = pl.DeviceIdType.MESH
CHAINED = (1,)
HEADS_PER_STEP = 8
CONTRACT_LAST = (((1,), (1,)), ((), ()))


def dot_last(left, right):
    return lax.dot_general(left, right, CONTRACT_LAST, preferred_element_type=jnp.float32)


def dot(left, right):
    return jnp.dot(left, right, preferred_element_type=jnp.float32)


def kernel(
    inner_size, outer_size,
    q_ref, k_ref, v_ref, g_ref, start_ref,
    dq_ref, dk_ref, dv_ref,
    qs, gs, ks, vs, kt, bias, early, stat, own_mask, prob, plow, ds, start_rows, own_sum, part, came,
    local_sem, send_sem, recv_sem,
):
    length = k_ref.shape[1]
    size = k_ref.shape[2]
    heads = q_ref.shape[2] // size
    scale = size ** (-0.5)
    blocks = inner_size * outer_size
    outer = lax.axis_index("outer")
    block = lax.axis_index("inner") * outer_size + outer

    def at(step):
        other = lax.rem(block + step + blocks, blocks)
        return (other // outer_size, lax.rem(other, outer_size))

    opens = outer == 0
    skips = jnp.logical_and(outer == outer_size - 2, block + 2 < blocks)
    passes = jnp.logical_and(outer < outer_size - 1, block >= 1)
    has_next = block + 1 < blocks

    barrier = pltpu.get_barrier_semaphore()

    def greet(step):
        pl.semaphore_signal(barrier, inc=1, device_id=at(step), device_id_type=MESH)

    pl.when(block >= 1)(lambda: greet(-1))
    pl.when(jnp.logical_and(opens, block >= 2))(lambda: greet(-2))

    loads = []

    def load(source, target):
        copy = pltpu.make_async_copy(source, target, local_sem.at[len(loads)])
        copy.start()
        loads.append(copy)

    load(start_ref, start_rows)
    load(k_ref.at[0], ks.at[pl.ds(0, length)])
    load(v_ref.at[0], vs.at[pl.ds(0, length)])
    for head in range(heads):
        load(q_ref.at[0, :, pl.ds(head * size, size)], qs.at[pl.ds(head * length, length)])
        load(g_ref.at[0, :, pl.ds(head * size, size)], gs.at[pl.ds(head * length, length)])

    own_rows, near_rows, far_rows = (pl.ds(tile * length, length) for tile in range(3))

    greeters = has_next.astype(jnp.int32) + skips.astype(jnp.int32)
    pl.when(has_next)(lambda: pl.semaphore_wait(barrier, greeters))
    sends = []

    def remote(source, target, step, give, take):
        return pltpu.make_async_remote_copy(
            src_ref=source, dst_ref=target,
            send_sem=send_sem.at[give], recv_sem=recv_sem.at[take],
            device_id=at(step), device_id_type=MESH,
        )

    def send(cond, *args):
        copy = remote(*args)
        pl.when(cond)(copy.start)
        sends.append((cond, copy))
        return copy

    key_near = send(has_next, k_ref.at[0], ks.at[near_rows], 1, 0, 0)
    key_far = send(skips, k_ref.at[0], ks.at[far_rows], 2, 2, 2)
    value_near = send(has_next, v_ref.at[0], vs.at[near_rows], 1, 1, 1)
    value_far = send(skips, v_ref.at[0], vs.at[far_rows], 2, 3, 3)

    def blank(rows):
        ks[rows] = jnp.zeros((length, size), jnp.bfloat16)
        vs[rows] = jnp.zeros((length, size), jnp.bfloat16)

    pl.when(block < 1)(lambda: blank(near_rows))
    pl.when(block < 2)(lambda: blank(far_rows))

    def no_part(slot):
        came[slot] = jnp.zeros((length, size), jnp.bfloat16)

    second, last = outer == 1, outer == outer_size - 1

    def expects(kind, tile):
        there = block + tile < blocks
        if kind not in CHAINED:
            return there
        return jnp.logical_and(there, jnp.logical_not(last if tile == 1 else second))

    for tile in (1, 2):
        for kind in range(2):
            missing = jnp.logical_not(expects(kind, tile))
            pl.when(missing)(functools.partial(no_part, 2 * kind + tile - 1))

    first = block * length
    key_at = lax.broadcasted_iota(jnp.int32, (length, length), 0)
    query_at = lax.broadcasted_iota(jnp.int32, (length, length), 1)
    causal = key_at <= query_at
    loads[0].wait()
    starts = start_rows[...]
    mixed_pos = first + key_at - jnp.where(causal, 0, 2 * length)
    bias[pl.ds(0, length)] = jnp.where(mixed_pos >= starts, 0.0, NEG_FILL)
    bias[pl.ds(length, length)] = jnp.where(first - length + key_at >= starts, 0.0, NEG_FILL)

    for copy in loads[1:]:
        copy.wait()

    own_mask[...] = jnp.where(causal, 1.0, 0.0).astype(jnp.bfloat16)

    def split(mixed):
        low = mixed.astype(jnp.bfloat16)
        own = low * own_mask[...]
        return own, low - own

    def merge(own, far):
        is_own = lax.broadcasted_iota(jnp.int32, (length, length), 0) <= lax.broadcasted_iota(
            jnp.int32, (length, length), 1
        )
        return jnp.where(is_own, own, far)

    def put(target, head, mixed, near):
        columns = pl.ds(pl.multiple_of(head * length, length), length)
        own, far = split(mixed)
        target[pl.ds(0, length), columns] = own
        target[pl.ds(length, length), columns] = near.astype(jnp.bfloat16)
        target[pl.ds(2 * length, length), columns] = far

    def over_heads(body):
        def step(index, carry):
            for inside in range(HEADS_PER_STEP):
                body(index * HEADS_PER_STEP + inside)
            return carry

        lax.fori_loop(0, heads // HEADS_PER_STEP, step, 0)

    def rows_of(head):
        return pl.ds(pl.multiple_of(head * length, length), length)

    def own_tile(head):
        early[0, head] = dot_last(ks[own_rows], qs[rows_of(head)]) + bias[own_rows]
        early[2, head] = dot_last(vs[own_rows], gs[rows_of(head)])

    def near_scores(head):
        scores = dot_last(ks[near_rows], qs[rows_of(head)]) + bias[near_rows]
        top = jnp.max(scores, axis=0, keepdims=True)
        weights = jnp.exp2((scores - top) * (scale * LOG2E))
        early[1, head] = weights
        stat[head, 0:1] = top
        stat[head, 1:2] = jnp.sum(weights, axis=0, keepdims=True)

    def near_grads(head):
        early[3, head] = dot_last(vs[near_rows], gs[rows_of(head)])

    over_heads(own_tile)
    pl.when(block >= 1)(key_near.wait_recv)
    send(passes, ks.at[near_rows], ks.at[far_rows], 1, 4, 2)
    over_heads(near_scores)
    pl.when(block >= 1)(value_near.wait_recv)
    send(passes, vs.at[near_rows], vs.at[far_rows], 1, 5, 3)
    over_heads(near_grads)
    pl.when(block >= 2)(key_far.wait_recv)

    def forward(head):
        far = dot_last(ks[far_rows], qs[rows_of(head)]) + bias[own_rows]
        mixed = merge(early[0, head], far)
        near_top = stat[head, 0:1]
        top = jnp.maximum(jnp.max(mixed, axis=0, keepdims=True), near_top)
        mixed = jnp.exp2((mixed - top) * (scale * LOG2E))
        shrink = jnp.exp2((near_top - top) * (scale * LOG2E))
        total = jnp.sum(mixed, axis=0, keepdims=True) + shrink * stat[head, 1:2]
        inverse = 1.0 / total
        mixed = mixed * inverse
        near = early[1, head] * (shrink * inverse)
        prob[head, pl.ds(0, length)] = mixed
        prob[head, pl.ds(length, length)] = near
        put(plow, head, mixed, near)

    over_heads(forward)

    gathers = jnp.where(second, 2, jnp.where(outer == outer_size - 2, 1, 0))

    def back(kind, tile, to_slot=None, step=None):
        slot = 2 * kind + tile - 1
        to_slot = slot if to_slot is None else to_slot
        step = -tile if step is None else step
        return remote(part.at[slot], came.at[to_slot], step, 6 + slot, 4 + to_slot)

    def give_back(weights, rows, kind):
        chained = kind in CHAINED
        lead = jnp.where(outer < 2, 1, 2) if chained else jnp.where(opens, 1, 2)
        for tile in (lead, 3 - lead):
            slot = 2 * kind + tile - 1
            from_rows = pl.ds(pl.multiple_of(tile * length, length), length)
            part[slot] = dot(weights[from_rows], rows[...]).astype(jnp.bfloat16)
            ready = block >= tile
            if not chained:
                pl.when(ready)(back(kind, tile).start)
                continue
            up = jnp.logical_and(opens, tile == 1)
            down = jnp.logical_and(last, tile == 2)
            aside = jnp.logical_or(up, down)
            step = jnp.where(aside, jnp.where(up, 1, -1), -tile)
            to_slot = jnp.where(aside, 4 + kind, slot)
            pl.when(jnp.logical_and(ready, tile != gathers))(back(kind, tile, to_slot, step).start)

    def settle(kind):
        slot = jnp.maximum(2 * kind + gathers - 1, 0)

        @pl.when(jnp.logical_and(gathers > 0, block >= gathers))
        def _():
            back(kind, 1, 4 + kind).wait_recv()
            both = part[slot].astype(jnp.float32) + came[4 + kind].astype(jnp.float32)
            part[slot] = both.astype(jnp.bfloat16)
            remote(part.at[slot], came.at[slot], -gathers, 6 + slot, 4 + slot).start()

    def take_back(kind):
        for tile in (1, 2):
            pl.when(expects(kind, tile))(back(kind, tile).wait_recv)

    give_back(plow, gs, 0)
    pl.when(block >= 2)(value_far.wait_recv)

    def backward(head):
        mixed = merge(early[2, head], dot_last(vs[far_rows], gs[rows_of(head)]))
        near = early[3, head]
        mixed_prob = prob[head, pl.ds(0, length)]
        near_prob = prob[head, pl.ds(length, length)]
        delta = jnp.sum(mixed_prob * mixed, axis=0, keepdims=True) + jnp.sum(
            near_prob * near, axis=0, keepdims=True
        )
        put(ds, head, mixed_prob * (mixed - delta), near_prob * (near - delta))

    over_heads(backward)
    give_back(ds, qs, 1)

    own_sum[0] = dot(plow[own_rows], gs[...])
    own_sum[1] = dot(ds[own_rows], qs[...])
    settle(1)
    kt[...] = ks[...].astype(jnp.float32).T.astype(jnp.bfloat16)

    for head in range(heads):
        turned = dot(kt[...], ds[:, pl.ds(head * length, length)]) * scale
        dq_ref[:, pl.ds(head * size, size)] = turned.T.astype(jnp.bfloat16)

    take_back(0)
    dv_ref[...] = (
        own_sum[0] + came[0].astype(jnp.float32) + came[1].astype(jnp.float32)
    ).astype(jnp.bfloat16)
    take_back(1)
    dk_ref[...] = (
        (own_sum[1] + came[2].astype(jnp.float32) + came[3].astype(jnp.float32)) * scale
    ).astype(jnp.bfloat16)
    for cond, copy in sends:
        pl.when(cond)(copy.wait_send)
    for kind in range(2):
        for tile in (1, 2):
            pl.when(block >= tile)(back(kind, tile).wait_send)


def write_out(dq_from, dk_from, dv_from, dq_ref, dk_ref, dv_ref, sem):
    pairs = ((dq_from, dq_ref), (dk_from, dk_ref), (dv_from, dv_ref))
    copies = [
        pltpu.make_async_copy(source, target.at[0], sem.at[which])
        for which, (source, target) in enumerate(pairs)
    ]
    for copy in copies:
        copy.start()
    for copy in copies:
        copy.wait()


def on_device(inner_size, outer_size, query_rows, key_rows, value_rows, out_grad, doc_start):
    length, size = key_rows.shape[1:]
    heads = query_rows.shape[2] // size
    low, wide = jnp.bfloat16, jnp.float32
    far = pl.BlockSpec(memory_space=pltpu.HBM)
    near = pl.BlockSpec(memory_space=pltpu.VMEM)
    given = (query_rows, key_rows, value_rows, out_grad, doc_start)
    results = pl.pallas_call(
        functools.partial(kernel, inner_size, outer_size),
        out_shape=(
            jax.ShapeDtypeStruct(query_rows.shape[1:], low),
            jax.ShapeDtypeStruct(key_rows.shape[1:], low),
            jax.ShapeDtypeStruct(value_rows.shape[1:], low),
        ),
        in_specs=[far] * 5,
        out_specs=(near, near, near),
        scratch_shapes=[
            pltpu.VMEM((heads * length, size), low),
            pltpu.VMEM((heads * length, size), low),
            pltpu.VMEM((3 * length, size), low),
            pltpu.VMEM((3 * length, size), low),
            pltpu.VMEM((size, 3 * length), low),
            pltpu.VMEM((2 * length, length), wide),
            pltpu.VMEM((4, heads, length, length), wide),
            pltpu.VMEM((heads, 8, length), wide),
            pltpu.VMEM((length, length), low),
            pltpu.VMEM((heads, 2 * length, length), wide),
            pltpu.VMEM((3 * length, heads * length), low),
            pltpu.VMEM((3 * length, heads * length), low),
            pltpu.VMEM((1, length), jnp.int32),
            pltpu.VMEM((2, length, size), wide),
            pltpu.VMEM((4, length, size), low),
            pltpu.VMEM((6, length, size), low),
            pltpu.SemaphoreType.DMA((3 + 2 * heads,)),
            pltpu.SemaphoreType.DMA((10,)),
            pltpu.SemaphoreType.DMA((10,)),
        ],
        compiler_params=pltpu.CompilerParams(
            collective_id=0, has_side_effects=True, vmem_limit_bytes=VMEM_BYTES
        ),
        name="window_attention_grad",
    )(*(pltpu.with_memory_space_constraint(rows, pltpu.HBM) for rows in given))
    return pl.pallas_call(
        write_out,
        out_shape=tuple(jax.ShapeDtypeStruct((1,) + result.shape, low) for result in results),
        in_specs=[near] * 3,
        out_specs=(far,) * 3,
        scratch_shapes=[pltpu.SemaphoreType.DMA((3,))],
        compiler_params=pltpu.CompilerParams(vmem_limit_bytes=1024 * 1024),
        name="write_out",
    )(*results)


def solution(mesh):
    rows = P("inner", "outer", None)
    return jax.shard_map(
        functools.partial(on_device, mesh.shape["inner"], mesh.shape["outer"]),
        mesh=mesh,
        in_specs=(rows, rows, rows, rows, P("inner", "outer")),
        out_specs=(rows, rows, rows),
        check_vma=False,
    )
```
